128 devices in a mesh: brick: 8 (over y, z_lo), gz: 16 (over x, z_hi, core).
Axes of the slice: x: 4, y: 4, z: 4 (z_hi: 2, z_lo: 2; z = z_hi * 2 + z_lo), core: 2. Of those that a mesh axis runs over, the one named last changes fastest.
Arguments:
- grad_field: float32 [5, 64, 1024, 512], P(None, 'brick', 'gz'), may hold values from -3 to 3
- alpha_coef: float32 [5, 64], P(None, 'brick'), may hold values from 0.3 to 0.4
- metric_inner: float32 [64, 1024], P('brick', 'gz'), may hold values from 0.5 to 2
- metric_outer: float32 [64, 1024], P('brick', 'gz'), may hold values from 0.5 to 2
Outputs:
- adjoint_field: float32 [5, 64, 1024, 512], P(None, 'brick', 'gz')
The draws below stay inside these ranges and needn't reach their ends.
All inputs are finite; a program needn't handle non-finite values.
Results may differ from the reference program's by a relative error of at most 0.00012.
Values sent between devices are 32-bit elements; how exact they have to be, the bound alone decides.
No kernel may reach another device: no remote copies, remote signals or barrier semaphores. Data moves between devices by JAX's collectives and lax.ppermute only.
A program may use at most 64 MiB of HBM per device.

```python
import math
import jax
import jax.numpy as jnp

F = 5
NY = 512
NX = 64
NZ = 1024


def steps_of(rng, shape, split, smallest, high):
    gain, own = 1.0, jax.random.fold_in(rng, 6)
    for position, shards_of in split:
        draws = jnp.exp(jax.random.uniform(jax.random.fold_in(own, position), (shards_of,), jnp.float32, smallest / len(split), high / len(split)))
        gain = gain * jnp.repeat(draws, shape[position] // shards_of).reshape([-1 if axis == position else 1 for axis in range(len(shape))])
    return gain


def normal_values(own_key, extent, scale, limit, cuts=(), kind=jnp.bfloat16):
    loudness = steps_of(own_key, extent, cuts, -0.22, 0.18) if cuts else 1.0
    values = jax.random.normal(own_key, extent, jnp.float32) * scale * loudness
    return jnp.minimum(jnp.maximum(values, -limit), limit).astype(kind)


def setup_inputs(seed: int = 0) -> dict:
    seeds = jax.random.split(jax.random.key(seed), 5)
    return {
        "grad_field": normal_values(seeds[0], (F, NX, NZ, NY), 0.5, 3.0, ((1, 8), (2, 16)), jnp.float32),
        "alpha_coef": jnp.clip(0.3 + 0.099999994 * jax.random.uniform(seeds[1], (F, NX), jnp.float32) ** steps_of(seeds[1], (F, NX), ((1, 8),), -0.2, 0.2), 0.3, 0.4),
        "metric_inner": jnp.clip(jnp.exp(math.log(2.0) - 1.3862944 * jax.random.uniform(seeds[2], (NX, NZ), jnp.float32) ** steps_of(seeds[2], (NX, NZ), ((0, 8), (1, 16)), -0.2, 0.2)), 0.5, 2.0),
        "metric_outer": jnp.clip(jnp.exp(math.log(2.0) - 1.3862944 * jax.random.uniform(seeds[3], (NX, NZ), jnp.float32) ** steps_of(seeds[3], (NX, NZ), ((0, 8), (1, 16)), -0.2, 0.2)), 0.5, 2.0),
    }


def solve_cyclic(values, alpha_coef):
    spectrum = jnp.fft.rfft(values, axis=2)
    wave = jnp.arange(NZ // 2 + 1).astype(jnp.float32)
    symbol = 1.0 + 2.0 * alpha_coef[:, :, None, None] * jnp.cos(2.0 * jnp.pi * wave / NZ)[None, None, :, None]
    return jnp.fft.irfft(spectrum / symbol, n=NZ, axis=2).astype(values.dtype)


def stencil_apply(values, alpha_coef):
    near_coef = (2.0 * (alpha_coef + 2.0) / 3.0)[:, :, None, None]
    far_coef = ((4.0 * alpha_coef - 1.0) / 3.0)[:, :, None, None]
    up_one = jnp.roll(values, -1, axis=2)
    down_one = jnp.roll(values, 1, axis=2)
    up_two = jnp.roll(values, -2, axis=2)
    down_two = jnp.roll(values, 2, axis=2)
    return -(near_coef * (up_one - down_one) * 0.5 + far_coef * (up_two - down_two) * 0.25)


def adjoint_pass(values, alpha_coef):
    return stencil_apply(solve_cyclic(values, alpha_coef), alpha_coef)


def reference(grad_field, alpha_coef, metric_inner, metric_outer):
    first = adjoint_pass(metric_inner[None, :, :, None] * grad_field, alpha_coef)
    padded = jnp.pad(first, ((0, 0), (1, 1), (0, 0), (0, 0)))
    smooth = first - 0.2 * (padded[:, 2:] - 2.0 * first + padded[:, :-2])
    middle = metric_outer[None, :, :, None] * smooth
    return adjoint_pass(middle, alpha_coef)
```

```python
import functools

import jax
import jax.numpy as jnp
from jax import lax
from jax.experimental import pallas as pl
from jax.experimental.pallas import tpu as pltpu
from jax.sharding import PartitionSpec as P

SMOOTH = 0.2
BF = jnp.bfloat16
F32 = jnp.float32
VMEM_LIMIT = 48 * 1024 * 1024


def iota(shape, axis):
    return lax.broadcasted_iota(jnp.int32, shape, axis)


def alternating(exponent):
    return (1 - 2 * (exponent % 2)).astype(F32)


def split(values):
    high = values.astype(BF)
    low = (values - high.astype(F32)).astype(BF)
    return high, low


def right_side(values):
    high, low = split(values)
    return jnp.concatenate([high, low, high, low], axis=0)


def left_side(matrix):
    high, low = split(matrix)
    return jnp.concatenate([high, low], axis=1)


def dot(left, right):
    return jnp.dot(left, right, preferred_element_type=F32)


def local_parts(cells):
    row = iota((cells, 2 * cells), 0)
    col = iota((cells, 2 * cells), 1) % cells
    step = col - row
    size = jnp.abs(step)
    sign = jnp.sign(step).astype(F32)
    return size.astype(F32), sign * alternating(size), jnp.where(size == 1, sign, 0.0)


def local_matrix(parts, coefs, metric):
    size, sign, near = parts
    log_ratio, beta, edge = coefs
    return (beta * (sign * jnp.exp(size * log_ratio)) - edge * near) * metric


def state_parts(cells):
    row = iota((16, 2 * cells), 0)
    col = iota((16, 2 * cells), 1) % cells
    reach = jnp.where(row == 0, cells - 1 - col, col)
    geometric = jnp.where((row == 0) | (row == 2), alternating(reach), 0.0)
    last = (row == 1) & (col == cells - 1)
    first = (row == 3) & (col == 0)
    return reach.astype(F32), geometric, jnp.where(last | first, 1.0, 0.0)


def state_matrix(parts, coefs, metric):
    reach, geometric, single = parts
    return (geometric * jnp.exp(reach * coefs[0]) + single) * metric


def border_parts(cells):
    row = iota((cells, 128), 0)
    lane = iota((cells, 128), 1)
    k = lane % 32
    after = k >= 16
    line = (k % 16) // 2
    single = (k % 2) == 1
    reach = jnp.where(after, cells - row, row + 1)
    side = jnp.where(after, 1.0, -1.0)
    geometric = jnp.where(single, 0.0, side * alternating(reach))
    beside = jnp.where(single & (reach == 1), -side, 0.0)
    return reach.astype(F32), geometric, beside, line, lane < 64


def border_matrix(parts, coefs, x):
    reach, geometric, beside, line, upper = parts
    log_ratio, beta, edge = coefs
    matrix = beta * (geometric * jnp.exp(reach * log_ratio)) + edge * beside
    matrix = jnp.where(line == x, matrix, 0.0)
    high = matrix.astype(BF).astype(F32)
    return jnp.where(upper, high, matrix - high).astype(BF)


def border_term(parts, coefs_of, left_ref, right_ref):
    states = jnp.concatenate([left_ref[0], right_ref[0]], axis=0)
    lines = left_ref.shape[1] // 2
    matrix = jnp.concatenate([border_matrix(parts, coefs_of(x), x) for x in range(lines)], axis=0)
    return dot(matrix, right_side(states))


def coefs_at(ref, index):
    return ref[0, index], ref[1, index], ref[2, index]


def states_kernel(coefs_ref, metric_ref, field_ref, ahead_ref, back_ref):
    f = pl.program_id(0)
    lines, cells = field_ref.shape[1], field_ref.shape[2]
    parts = state_parts(cells)
    for x in range(lines):
        coefs = coefs_at(coefs_ref, f * lines + x)
        matrix = state_matrix(parts, coefs, metric_ref[x : x + 1])
        rows = dot(left_side(matrix), right_side(field_ref[0, x]))
        ahead_ref[0, 2 * x : 2 * x + 2] = rows[0:2]
        back_ref[0, 2 * x : 2 * x + 2] = rows[2:4]


def middle_kernel(
    coefs_ref, halo_coefs_ref, inner_ref, outer_ref, halo_outer_ref, field_ref, left_ref, right_ref,
    out_ref, ahead_ref, back_ref, below_ref, above_ref, border_scr, first_scr,
):
    f = pl.program_id(0)
    lines, cells = field_ref.shape[1], field_ref.shape[2]
    locals_ = local_parts(cells)
    states = state_parts(cells)
    coefs_of = lambda x: coefs_at(coefs_ref, f * lines + x)
    border_scr[...] = border_term(border_parts(cells), coefs_of, left_ref, right_ref)
    for x in range(lines):
        matrix = local_matrix(locals_, coefs_of(x), inner_ref[x : x + 1])
        first_scr[x] = dot(left_side(matrix), right_side(field_ref[0, x])) + border_scr[cells * x : cells * (x + 1)]
    for x in range(lines):
        middle = (1.0 + 2.0 * SMOOTH) * first_scr[x]
        if x > 0:
            middle = middle - SMOOTH * first_scr[x - 1]
        if x < lines - 1:
            middle = middle - SMOOTH * first_scr[x + 1]
        metric = outer_ref[x : x + 1]
        left = jnp.concatenate(
            [
                left_side(local_matrix(locals_, coefs_of(x), metric)),
                left_side(state_matrix(states, coefs_of(x), metric)),
            ],
            axis=0,
        )
        rows = dot(left, right_side(middle))
        out_ref[0, x] = rows[:cells]
        ahead_ref[0, 2 * x : 2 * x + 2] = rows[cells : cells + 2]
        back_ref[0, 2 * x : 2 * x + 2] = rows[cells + 2 : cells + 4]
    for side, x, ref in ((0, 0, below_ref), (1, lines - 1, above_ref)):
        coefs = coefs_at(halo_coefs_ref, 2 * f + side)
        matrix = state_matrix(states, coefs, -SMOOTH * halo_outer_ref[side : side + 1])
        rows = dot(left_side(matrix), right_side(first_scr[x]))
        ref[0] = rows[0:4]


def border_kernel(coefs_ref, part_ref, left_ref, right_ref, out_ref):
    f = pl.program_id(0)
    lines, cells = part_ref.shape[1], part_ref.shape[2]
    coefs_of = lambda x: coefs_at(coefs_ref, f * lines + x)
    border = border_term(border_parts(cells), coefs_of, left_ref, right_ref)
    for x in range(lines):
        out_ref[0, x] = part_ref[0, x] + border[cells * x : cells * (x + 1)]


def edge_kernel(
    lines, coefs_ref, halo_coefs_ref, halo_inner_ref, outer_ref, part_ref, halo_ref, rows_ref, out_ref, state_scr
):
    side, f = pl.program_id(0), pl.program_id(1)
    cells = part_ref.shape[2]
    x = side * (lines - 1)
    locals_ = local_parts(cells)
    halo_coefs = coefs_at(halo_coefs_ref, 2 * f + side)
    state_scr[...] = jnp.zeros_like(state_scr)
    state_scr[0:2] = rows_ref[0, 0, 0:2]
    state_scr[16:18] = rows_ref[0, 0, 2:4]
    inner = halo_inner_ref[pl.ds(side, 1)]
    outer = outer_ref[pl.ds(x, 1)]
    first = dot(left_side(local_matrix(locals_, halo_coefs, inner)), right_side(halo_ref[0, 0]))
    first = first + dot(border_matrix(border_parts(cells), halo_coefs, 0), right_side(state_scr[...]))
    matrix = local_matrix(locals_, coefs_at(coefs_ref, f * lines + x), -SMOOTH * outer)
    out_ref[0, 0] = part_ref[0, 0] + dot(left_side(matrix), right_side(first))


SMEM = pl.BlockSpec(memory_space=pltpu.SMEM)
WHOLE = pl.BlockSpec(memory_space=pltpu.VMEM)


def coef_table(alpha_coef):
    safe = jnp.where(alpha_coef > 0.0, alpha_coef, 0.25)
    ratio = 2.0 * safe / (1.0 + jnp.sqrt(1.0 - 4.0 * safe * safe))
    edge = (4.0 * safe - 1.0) / (12.0 * safe)
    beta = ((safe + 2.0) / 3.0 - edge) / safe
    return jnp.stack([jnp.log(ratio).reshape(-1), beta.reshape(-1), edge.reshape(-1)])


def twice(metric):
    return jnp.concatenate([metric, metric], axis=1)


def body(grad_field, alpha_coef, metric_inner, metric_outer):
    fields, lines, cells, width = grad_field.shape
    bricks, rings = lax.axis_size("brick"), lax.axis_size("gz")
    up_x = [(i, i + 1) for i in range(bricks - 1)]
    down_x = [(i + 1, i) for i in range(bricks - 1)]
    up_z = [(i, (i + 1) % rings) for i in range(rings)]
    down_z = [((i + 1) % rings, i) for i in range(rings)]

    def both(x_pairs, z_pairs):
        return [(a * rings + c, b * rings + d) for a, b in x_pairs for c, d in z_pairs]

    def facts(x):
        return jnp.concatenate([alpha_coef[:, x], metric_inner[x], metric_outer[x]])[None]

    lower = lax.ppermute(facts(lines - 1), "brick", up_x)
    upper = lax.ppermute(facts(0), "brick", down_x)
    halo_facts = jnp.concatenate([lower, upper], axis=0)
    halo_coefs = coef_table(halo_facts[:, :fields].T)
    halo_inner = twice(halo_facts[:, fields : fields + cells])
    halo_outer = twice(halo_facts[:, fields + cells :])
    coefs = coef_table(alpha_coef)
    inner, outer = twice(metric_inner), twice(metric_outer)

    params = pltpu.CompilerParams(vmem_limit_bytes=VMEM_LIMIT)
    block = pl.BlockSpec((1, lines, cells, width), lambda f: (f, 0, 0, 0))
    states = pl.BlockSpec((1, 2 * lines, width), lambda f: (f, 0, 0))
    four = pl.BlockSpec((1, 4, width), lambda f: (f, 0, 0))
    states_shape = jax.ShapeDtypeStruct((fields, 2 * lines, width), F32)
    four_shape = jax.ShapeDtypeStruct((fields, 4, width), F32)
    whole_shape = jax.ShapeDtypeStruct(grad_field.shape, F32)

    ahead, back = pl.pallas_call(
        states_kernel,
        grid=(fields,),
        in_specs=[SMEM, WHOLE, block],
        out_specs=[states, states],
        out_shape=[states_shape, states_shape],
        compiler_params=params,
        name="states",
    )(coefs, inner, grad_field)
    left = lax.ppermute(ahead, "gz", up_z)
    right = lax.ppermute(back, "gz", down_z)

    cut = 3
    halo_lower = [lax.ppermute(grad_field[:cut, lines - 1], "brick", up_x)]
    halo_upper = [lax.ppermute(grad_field[:cut, 0], "brick", down_x)]

    part, ahead, back, below, above = pl.pallas_call(
        middle_kernel,
        grid=(fields,),
        in_specs=[SMEM, SMEM, WHOLE, WHOLE, WHOLE, block, states, states],
        out_specs=[block, states, states, four, four],
        out_shape=[whole_shape, states_shape, states_shape, four_shape, four_shape],
        scratch_shapes=[
            pltpu.VMEM((lines * cells, width), F32),
            pltpu.VMEM((lines, cells, width), F32),
        ],
        compiler_params=params,
        name="middle",
    )(coefs, halo_coefs, inner, outer, halo_outer, grad_field, left, right)

    left2 = lax.ppermute(ahead, "gz", up_z)
    right2 = lax.ppermute(back, "gz", down_z)
    axes = ("brick", "gz")
    corner = {
        (0, 0): lax.ppermute(above[:, 0:2], axes, both(up_x, up_z)),
        (0, 1): lax.ppermute(below[:, 0:2], axes, both(down_x, up_z)),
        (1, 0): lax.ppermute(above[:, 2:4], axes, both(up_x, down_z)),
        (1, 1): lax.ppermute(below[:, 2:4], axes, both(down_x, down_z)),
    }

    def with_rows(tail, rows):
        return jnp.concatenate([tail.reshape(-1, width), rows.reshape(-1, width)], axis=0)

    tail_lower = lax.ppermute(
        with_rows(grad_field[cut:, lines - 1], jnp.concatenate([left[:, -2:], right[:, -2:]], axis=1)), "brick", up_x
    )
    tail_upper = lax.ppermute(
        with_rows(grad_field[cut:, 0], jnp.concatenate([left[:, :2], right[:, :2]], axis=1)), "brick", down_x
    )

    def add_corners(rows, z):
        gap = jnp.zeros((fields, 2 * lines - 4, width), F32)
        return rows + jnp.concatenate([corner[z, 0], gap, corner[z, 1]], axis=1)

    part = pl.pallas_call(
        border_kernel,
        grid=(fields,),
        in_specs=[SMEM, block, states, states],
        out_specs=block,
        out_shape=whole_shape,
        input_output_aliases={1: 0},
        compiler_params=params,
        name="border",
    )(coefs, part, add_corners(left2, 0), add_corners(right2, 1))

    count = (fields - cut) * cells
    halo = jnp.stack(
        [
            jnp.concatenate([halo_lower[0], tail_lower[:count].reshape(fields - cut, cells, width)], axis=0),
            jnp.concatenate([halo_upper[0], tail_upper[:count].reshape(fields - cut, cells, width)], axis=0),
        ]
    )
    rows = jnp.stack([tail_lower[count:], tail_upper[count:]]).reshape(2, fields, 4, width)
    edge = pl.BlockSpec((1, 1, cells, width), lambda side, f: (f, side * (lines - 1), 0, 0))
    return pl.pallas_call(
        functools.partial(edge_kernel, lines),
        grid=(2, fields),
        in_specs=[
            SMEM,
            SMEM,
            WHOLE,
            WHOLE,
            edge,
            pl.BlockSpec((1, 1, cells, width), lambda side, f: (side, f, 0, 0)),
            pl.BlockSpec((1, 1, 4, width), lambda side, f: (side, f, 0, 0)),
        ],
        out_specs=edge,
        out_shape=whole_shape,
        input_output_aliases={4: 0},
        scratch_shapes=[pltpu.VMEM((32, width), F32)],
        compiler_params=params,
        name="edge",
    )(coefs, halo_coefs, halo_inner, outer, part, halo, rows)


def solution(mesh):
    placed = (P(None, "brick", "gz", None), P(None, "brick"), P("brick", "gz"), P("brick", "gz"))
    return jax.shard_map(
        body, mesh=mesh, in_specs=placed, out_specs=P(None, "brick", "gz", None), check_vma=False
    )
```

```python
import jax
import jax.numpy as jnp
from jax import lax
from jax.experimental import pallas as pl
from jax.experimental.pallas import tpu as pltpu
from jax.sharding import PartitionSpec as P

SMOOTH = 0.2
BF = jnp.bfloat16
F32 = jnp.float32
GRANT = 54
AHEAD = 3
CUT = 2


def iota(shape, axis):
    return lax.broadcasted_iota(jnp.int32, shape, axis)


def alternating(exponent):
    return (1 - 2 * (exponent & 1)).astype(F32)


def split(values):
    high = values.astype(BF)
    low = (values - high.astype(F32)).astype(BF)
    return high, low


def right_side(values):
    high, low = split(values)
    return jnp.concatenate([high, low, high], axis=0)


def left_side(matrix):
    high, low = split(matrix)
    return jnp.concatenate([high, low[:, : matrix.shape[1] // 2]], axis=1)


def dot(left, right):
    return jnp.dot(left, right, preferred_element_type=F32)


def coefs_of(alpha):
    safe = jnp.where(alpha > 0.0, alpha, 0.25)
    ratio = 2.0 * safe / (1.0 + jnp.sqrt(1.0 - 4.0 * safe * safe))
    edge = (4.0 * safe - 1.0) / (12.0 * safe)
    beta = ((safe + 2.0) / 3.0 - edge) / safe
    return jnp.log(ratio), beta, edge


def alpha_column(row):
    n = row.shape[1]
    return jnp.sum(jnp.where(iota((n, n), 0) == iota((n, n), 1), row, 0.0), axis=1, keepdims=True)


def at(coefs, x):
    return tuple(c[x : x + 1] for c in coefs)


def local_parts(cells):
    row = iota((cells, 2 * cells), 0)
    col = iota((cells, 2 * cells), 1) & (cells - 1)
    step = col - row
    size = jnp.abs(step)
    sign = jnp.where(step > 0, 1.0, jnp.where(step < 0, -1.0, 0.0))
    return size.astype(F32), sign * alternating(size), jnp.where(size == 1, sign, 0.0)


def local_matrix(parts, coefs):
    size, sign, near = parts
    log_ratio, beta, edge = coefs
    return beta * (sign * jnp.exp(size * log_ratio)) - edge * near


def state_parts(cells):
    row = iota((16, 2 * cells), 0)
    col = iota((16, 2 * cells), 1) & (cells - 1)
    reach = jnp.where(row == 0, cells - 1 - col, col)
    geometric = jnp.where((row == 0) | (row == 2), alternating(reach), 0.0)
    last = (row == 1) & (col == cells - 1)
    first = (row == 3) & (col == 0)
    return reach.astype(F32), geometric, jnp.where(last | first, 1.0, 0.0)


def state_matrix(parts, coefs, metric):
    reach, geometric, single = parts
    return (geometric * jnp.exp(reach * coefs[0]) + single) * metric


def border_matrix(cells, coefs, after, single):
    row = iota((cells, 128), 0)
    log_ratio, beta, edge = coefs
    reach = jnp.where(after, cells - row, row + 1)
    side = jnp.where(after, 1.0, -1.0)
    geometric = side * alternating(reach) * jnp.exp(reach.astype(F32) * log_ratio)
    beside = jnp.where(reach == 1, -side, 0.0)
    return jnp.where(single, edge * beside, beta * geometric)


def rows_left(matrix):
    high = matrix.astype(BF).astype(F32)
    return jnp.where(iota(matrix.shape, 1) < 64, high, matrix - high).astype(BF)


def pick(values, index_of_lane, alphas):
    lanes = jnp.zeros((1, 128), F32)
    for n in range(values):
        lanes = jnp.where(index_of_lane == n, alphas(n), lanes)
    return lanes


def doubled(row):
    return jnp.concatenate([row, row], axis=1)


def is_odd(axis):
    return lax.rem(lax.axis_index(axis), 2) == 1


def halo_facts(near_ref, far_ref, side, fields, lines, cells):
    x = 0 if side else lines - 1
    near = is_odd("brick") == (side == 0)
    facts = jnp.where(near, near_ref[...], far_ref[...])
    alphas = facts[0:fields, 128:256]
    alpha = jnp.sum(jnp.where(iota(alphas.shape, 1) == x, alphas, 0.0), axis=1, keepdims=True)
    return alpha, doubled(facts[0:1, 0:cells]), doubled(facts[0:1, cells : 2 * cells])


def put_rows(near_ref, far_ref, index, odd, ahead, back):
    near_ref[index] = jnp.where(odd, back, ahead)
    far_ref[index] = jnp.where(odd, ahead, back)


def fetch(field_in, field_scr, sem):
    fields, lines = field_scr.shape[:2]

    def copies(f):
        return [pltpu.make_async_copy(field_in.at[f, x], field_scr.at[f, x], sem.at[f, x]) for x in range(lines)]

    for f in range(AHEAD):
        for copy in copies(f):
            copy.start()

    def ready(f):
        for copy in copies(f):
            copy.wait()

        @pl.when(f + AHEAD < fields)
        def _():
            for copy in copies(f + AHEAD):
                copy.start()

    return ready


def fetch_small(pairs, sem):
    copies = [pltpu.make_async_copy(source, target, sem.at[n]) for n, (source, target) in enumerate(pairs)]
    for copy in copies:
        copy.start()
    return copies


def open_kernel(
    alpha_in, inner_in, outer_in, field_in,
    near_ref, far_ref, edge_near_ref, edge_far_ref, facts_near_ref, facts_far_ref, alpha_ref, inner_ref, outer_ref,
    late_near_ref, late_far_ref, field_ref, sem, field_sem,
):
    fields, lines, cells = field_ref.shape[:3]
    odd_x, odd_z = is_odd("brick"), is_odd("gz")
    small = fetch_small([(alpha_in, alpha_ref), (inner_in, inner_ref), (outer_in, outer_ref)], sem)
    ready = fetch(field_in, field_ref, field_sem)
    for copy in small:
        copy.wait()
    parts = state_parts(cells)

    @pl.loop(0, fields)
    def _(f):
        coefs = coefs_of(alpha_column(alpha_ref[pl.ds(f, 1)]))
        ready(f)
        for x in range(lines):
            matrix = state_matrix(parts, at(coefs, x), doubled(inner_ref[x : x + 1]))
            rows = dot(left_side(matrix), right_side(field_ref[f, x]))
            put_rows(near_ref, far_ref, (f, slice(2 * x, 2 * x + 2)), odd_z, rows[0:2], rows[2:4])

    for f in range(fields):
        near, far, n = (edge_near_ref, edge_far_ref, f) if f < CUT else (late_near_ref, late_far_ref, f - CUT)
        low, high = field_ref[f, 0], field_ref[f, lines - 1]
        near[n] = jnp.where(odd_x, low, high)
        far[n] = jnp.where(odd_x, high, low)
    metrics = jnp.concatenate([inner_ref[...], outer_ref[...]], axis=1)
    for ref, low in ((facts_near_ref, odd_x), (facts_far_ref, jnp.logical_not(odd_x))):
        ref[...] = jnp.zeros_like(ref)
        ref[0:1, 0 : 2 * cells] = jnp.where(low, metrics[0:1], metrics[lines - 1 :])
        ref[0:fields, 128 : 128 + lines] = alpha_ref[...]


def border_term(lines, cells, alphas, f, near_ref, far_ref):
    odd = is_odd("gz")
    near, far = near_ref[f, : 2 * lines], far_ref[f, : 2 * lines]
    states = jnp.concatenate([jnp.where(odd, near, far), jnp.where(odd, far, near)], axis=0)
    k = iota((1, 128), 1) & 31
    line = (k & 15) >> 1
    lane_coefs = coefs_of(pick(lines, line, lambda x: alphas[x : x + 1]))
    matrix = rows_left(border_matrix(cells, lane_coefs, k >= 16, (k & 1) == 1)).astype(F32)
    left = jnp.concatenate([jnp.where(line == x, matrix, 0.0).astype(BF) for x in range(lines)], axis=0)
    high, low = split(states)
    return dot(left, jnp.concatenate([high, low, high, low], axis=0))


def middle_kernel(
    alpha_ref, inner_ref, outer_ref, field_ref, near_ref, far_ref,
    out_ref, near_out_ref, far_out_ref, edge_ref, border_scr, first_scr, local_scr,
):
    fields, lines, cells = field_ref.shape[:3]
    parts = local_parts(cells)
    states = state_parts(cells)
    odd = is_odd("gz")

    @pl.loop(0, fields)
    def _(f):
        alphas = alpha_column(alpha_ref[pl.ds(f, 1)])
        coefs = coefs_of(alphas)
        border_scr[...] = border_term(lines, cells, alphas, f, near_ref, far_ref)
        for x in range(lines):
            matrix = local_matrix(parts, at(coefs, x))
            local_scr[x] = matrix
            left = left_side(matrix * doubled(inner_ref[x : x + 1]))
            first_scr[x] = dot(left, right_side(field_ref[f, x])) + border_scr[cells * x : cells * (x + 1)]
        for x in range(lines):
            middle = (1.0 + 2.0 * SMOOTH) * first_scr[x]
            if x > 0:
                middle = middle - SMOOTH * first_scr[x - 1]
            if x < lines - 1:
                middle = middle - SMOOTH * first_scr[x + 1]
            metric = doubled(outer_ref[x : x + 1])
            left = jnp.concatenate(
                [left_side(local_scr[x] * metric), left_side(state_matrix(states, at(coefs, x), metric))], axis=0
            )
            rows = dot(left, right_side(middle))
            out_ref[f, x] = rows[:cells]
            put_rows(
                near_out_ref, far_out_ref, (f, slice(2 * x, 2 * x + 2)), odd,
                rows[cells : cells + 2], rows[cells + 2 : cells + 4],
            )
        edge_ref[f, 0] = first_scr[0]
        edge_ref[f, 1] = first_scr[lines - 1]


def corner_kernel(near_x_ref, far_x_ref, edge_ref, near_ref, far_ref, near_out_ref, far_out_ref):
    fields, cells, lines = edge_ref.shape[0], edge_ref.shape[2], near_ref.shape[1] // 2
    states = state_parts(cells)
    odd = is_odd("gz")
    for f in range(fields):
        near_out_ref[f, 0 : 2 * lines] = near_ref[f]
        far_out_ref[f, 0 : 2 * lines] = far_ref[f]
    for side in range(2):
        alphas, _, metric = halo_facts(near_x_ref, far_x_ref, side, fields, lines, cells)
        coefs = coefs_of(alphas)
        for f in range(fields):
            matrix = state_matrix(states, at(coefs, f), -SMOOTH * metric)
            rows = dot(left_side(matrix), right_side(edge_ref[f, side]))
            place = 2 * lines + 2 * side
            put_rows(near_out_ref, far_out_ref, (f, slice(place, place + 2)), odd, rows[0:2], rows[2:4])


def prepare_kernel(alpha_ref, outer_ref, near_x_ref, far_x_ref, cells_ref, rows_ref):
    fields, lines = alpha_ref.shape
    cells = outer_ref.shape[1]
    parts = local_parts(cells)
    k = iota((1, 128), 1) & 63
    own = k >= 4 * fields
    field = jnp.where(own, k - 4 * fields, k) >> 2

    @pl.loop(0, fields)
    def _(f):
        coefs = coefs_of(alpha_column(alpha_ref[pl.ds(f, 1)]))
        for side, x in ((0, 0), (1, lines - 1)):
            alphas, metric, _ = halo_facts(near_x_ref, far_x_ref, side, fields, lines, cells)
            own_alphas = jnp.sum(jnp.where(iota((fields, lines), 1) == x, alpha_ref[...], 0.0), axis=1, keepdims=True)
            alpha = jnp.sum(jnp.where(iota((fields, 1), 0) == f, alphas, 0.0), axis=0, keepdims=True)
            outer = left_side(local_matrix(parts, at(coefs, x)) * (-SMOOTH * doubled(outer_ref[x : x + 1])))
            inner = local_matrix(parts, coefs_of(alpha)) * metric
            cells_ref[f, side] = left_side(dot(outer, right_side(inner)))
            halo_lanes = pick(fields, field, lambda n: alphas[n : n + 1])
            own_lanes = pick(fields, field, lambda n: own_alphas[n : n + 1])
            border = border_matrix(cells, coefs_of(jnp.where(own, own_lanes, halo_lanes)), (k & 2) == 2, (k & 1) == 1)
            border = jnp.where(field == f, border, 0.0)
            passed = dot(outer, right_side(jnp.where(own, 0.0, border)))
            rows_ref[f, side] = left_side(passed + jnp.where(own, border, 0.0))


def gather_kernel(near1_ref, far1_ref, near2_ref, far2_ref, near_ref, far_ref):
    fields, lines = near1_ref.shape[0], near1_ref.shape[1] // 2
    odd_z, odd_x = is_odd("gz"), is_odd("brick")
    for half, near, far in ((0, near1_ref, far1_ref), (1, near2_ref, far2_ref)):
        for f in range(fields):
            rows = []
            for side, x in ((0, 0), (1, lines - 1)):
                place = 2 * x if half == 0 else 2 * lines + 2 * side
                one, two = near[f, place : place + 2], far[f, place : place + 2]
                rows.append(jnp.concatenate([jnp.where(odd_z, one, two), jnp.where(odd_z, two, one)], axis=0))
            at_row = 4 * (fields * half + f)
            near_ref[at_row : at_row + 4] = jnp.where(odd_x, rows[0], rows[1])
            far_ref[at_row : at_row + 4] = jnp.where(odd_x, rows[1], rows[0])


def border_kernel(alpha_ref, part_ref, near_ref, far_ref, out_ref, edge_ref, stage, sem):
    fields, lines, cells = part_ref.shape[:3]

    def copies(f):
        return [pltpu.make_async_copy(stage.at[f, x], out_ref.at[f, x], sem.at[f, x]) for x in range(lines)]

    @pl.loop(0, fields)
    def _(f):
        border = border_term(lines, cells, alpha_column(alpha_ref[pl.ds(f, 1)]), f, near_ref, far_ref)
        for x in range(lines):
            value = part_ref[f, x] + border[cells * x : cells * (x + 1)]
            stage[f, x] = value
            if x == 0 or x == lines - 1:
                edge_ref[f, 0 if x == 0 else 1] = value
        for copy in copies(f):
            copy.start()

    @pl.loop(0, fields)
    def _(f):
        for copy in copies(f):
            copy.wait()


def by_side(near_ref, far_ref, index):
    odd = is_odd("brick")
    near, far = near_ref[index], far_ref[index]
    return jnp.where(odd, near, far), jnp.where(odd, far, near)


def late_kernel(
    cells_ref, rows_ref, edge_ref, near1_ref, far1_ref, near2_ref, far2_ref, near_rows_ref, far_rows_ref, _,
    out_ref, state_scr, term_scr, stage, sem,
):
    fields, cells, lines = edge_ref.shape[0], edge_ref.shape[2], out_ref.shape[1]
    copies = []
    for side, rows in enumerate(by_side(near_rows_ref, far_rows_ref, Ellipsis)):
        state_scr[...] = jnp.zeros_like(state_scr)
        state_scr[0 : 8 * fields] = rows
        left = jnp.concatenate([rows_ref[f, side] for f in range(fields)], axis=0)
        term_scr[side] = dot(left, right_side(state_scr[...]))
    for f in range(fields):
        pieces = by_side(near1_ref, far1_ref, f) if f < CUT else by_side(near2_ref, far2_ref, f - CUT)
        for side, halo in enumerate(pieces):
            term = edge_ref[f, side] + term_scr[side, cells * f : cells * (f + 1)]
            stage[f, side] = term + dot(cells_ref[f, side], right_side(halo))
            copies.append(pltpu.make_async_copy(stage.at[f, side], out_ref.at[f, side * (lines - 1)], sem.at[f, side]))
            copies[-1].start()
    for copy in copies:
        copy.wait()


WHOLE = pl.BlockSpec(memory_space=pltpu.VMEM)
ANY = pl.BlockSpec(memory_space=pl.ANY)
HBM = pl.BlockSpec(memory_space=pltpu.HBM)


def call(kernel, limit, ins, out_shape, outs=WHOLE, **options):
    def run(*args):
        return pl.pallas_call(
            kernel,
            in_specs=ins,
            out_specs=outs if isinstance(outs, list) else jax.tree.map(lambda _: outs, out_shape),
            out_shape=out_shape,
            compiler_params=pltpu.CompilerParams(vmem_limit_bytes=limit * 1024 * 1024),
            **options,
        )(*args)

    return run


def swap(axis, near, far):
    count = lax.axis_size(axis)
    ends = count if axis == "gz" else count - 1
    pairs = {"near": [(i, i + 1) for i in range(0, count - 1, 2)], "far": [(i, (i + 1) % count) for i in range(1, ends, 2)]}
    moved = {}
    for kind, value in (("far", far), ("near", near)):
        both = [p for a, b in pairs[kind] for p in ((a, b), (b, a))]
        moved[kind] = lax.ppermute(value, axis, both)
    return moved["near"], moved["far"]


def steps(grad_field, alpha_coef, metric_inner, metric_outer):
    fields, lines, cells, width = grad_field.shape

    def shape(*dims, kind=F32):
        return pltpu.VMEM(dims, kind)

    whole = jax.ShapeDtypeStruct(grad_field.shape, F32)

    rows = shape(fields, 2 * lines, width)
    edge, tail = shape(CUT, cells, width), shape(fields - CUT, cells, width)
    facts, edges = shape(8, 256), shape(fields, 2, cells, width)
    inputs = (alpha_coef, metric_inner, metric_outer, grad_field)
    held = [pltpu.SemaphoreType.DMA((3,)), pltpu.SemaphoreType.DMA((fields, lines))]
    near, far, edge_near, edge_far, facts_near, facts_far, alpha, inner, outer, tail_near, tail_far, field = call(
        open_kernel,
        GRANT,
        [HBM] * 4,
        [rows, rows, edge, edge, facts, facts, *(shape(*a.shape) for a in inputs[:3]), tail, tail, shape(*grad_field.shape)],
        scratch_shapes=held,
    )(*inputs)
    near_one, far_one = swap("gz", near, far)
    near1, far1 = swap("brick", edge_near, edge_far)
    near0, far0 = swap("brick", facts_near, facts_far)

    part, near, far, first = call(
        middle_kernel,
        8,
        [WHOLE] * 6,
        [shape(*grad_field.shape), rows, rows, edges],
        scratch_shapes=[
            pltpu.VMEM((lines * cells, width), F32),
            pltpu.VMEM((lines, cells, width), F32),
            pltpu.VMEM((lines, cells, 2 * cells), F32),
        ],
    )(alpha, inner, outer, field, near_one, far_one)
    rows = shape(fields, 2 * lines + 4, width)
    near, far = call(corner_kernel, 4, [WHOLE] * 5, [rows, rows])(near0, far0, first, near, far)
    near_two, far_two = swap("gz", near, far)
    near2, far2 = swap("brick", tail_near, tail_far)

    matrices = shape(fields, 2, cells, 3 * cells, kind=BF)
    cell_matrix, row_matrix = call(prepare_kernel, 4, [WHOLE] * 4, [matrices, matrices])(alpha, outer, near0, far0)

    rows = shape(8 * fields, width)
    near, far = call(gather_kernel, 2, [WHOLE] * 4, [rows, rows])(near_one, far_one, near_two, far_two)
    near3, far3 = swap("brick", near, far)

    out, edge = call(
        border_kernel,
        16,
        [WHOLE] * 4,
        [whole, edges],
        outs=[HBM, WHOLE],
        scratch_shapes=[pltpu.VMEM(grad_field.shape, F32), pltpu.SemaphoreType.DMA((fields, lines))],
    )(alpha, part, near_two, far_two)

    return call(
        late_kernel,
        8,
        [WHOLE] * 9 + [HBM],
        whole,
        outs=HBM,
        input_output_aliases={9: 0},
        scratch_shapes=[
            pltpu.VMEM((cells, width), F32),
            pltpu.VMEM((2, fields * cells, width), F32),
            pltpu.VMEM((fields, 2, cells, width), F32),
            pltpu.SemaphoreType.DMA((fields, 2)),
        ],
    )(cell_matrix, row_matrix, edge, near1, far1, near2, far2, near3, far3, out)


def solution(mesh):
    placed = (P(None, "brick", "gz", None), P(None, "brick"), P("brick", "gz"), P("brick", "gz"))
    return jax.shard_map(steps, mesh=mesh, in_specs=placed, out_specs=P(None, "brick", "gz", None), check_vma=False)
```

```python
import jax
import jax.numpy as jnp
from jax import lax
from jax.experimental import pallas as pl
from jax.experimental.pallas import tpu as pltpu
from jax.sharding import PartitionSpec as P

SMOOTH = 0.2
BF = jnp.bfloat16
F32 = jnp.float32
GRANT = 54
AHEAD = 3


def iota(shape, axis):
    return lax.broadcasted_iota(jnp.int32, shape, axis)


def alternating(exponent):
    return (1 - 2 * (exponent & 1)).astype(F32)


def split(values):
    high = values.astype(BF)
    low = (values - high.astype(F32)).astype(BF)
    return high, low


def right_side(values):
    high, low = split(values)
    return jnp.concatenate([high, low, high], axis=0)


def left_side(matrix):
    high, low = split(matrix)
    return jnp.concatenate([high, low[:, : matrix.shape[1] // 2]], axis=1)


def dot(left, right):
    return jnp.dot(left, right, preferred_element_type=F32)


def coefs_of(alpha):
    safe = jnp.where(alpha > 0.0, alpha, 0.25)
    ratio = 2.0 * safe / (1.0 + jnp.sqrt(1.0 - 4.0 * safe * safe))
    edge = (4.0 * safe - 1.0) / (12.0 * safe)
    beta = ((safe + 2.0) / 3.0 - edge) / safe
    return jnp.log(ratio), beta, edge


def alpha_column(row):
    n = row.shape[1]
    return jnp.sum(jnp.where(iota((n, n), 0) == iota((n, n), 1), row, 0.0), axis=1, keepdims=True)


def at(coefs, x):
    return tuple(c[x : x + 1] for c in coefs)


def local_parts(cells):
    row = iota((cells, 2 * cells), 0)
    col = iota((cells, 2 * cells), 1) & (cells - 1)
    step = col - row
    size = jnp.abs(step)
    sign = jnp.where(step > 0, 1.0, jnp.where(step < 0, -1.0, 0.0))
    return size.astype(F32), sign * alternating(size), jnp.where(size == 1, sign, 0.0)


def local_matrix(parts, coefs):
    size, sign, near = parts
    log_ratio, beta, edge = coefs
    return beta * (sign * jnp.exp(size * log_ratio)) - edge * near


def state_parts(cells):
    row = iota((16, 2 * cells), 0)
    col = iota((16, 2 * cells), 1) & (cells - 1)
    reach = jnp.where(row == 0, cells - 1 - col, col)
    geometric = jnp.where((row == 0) | (row == 2), alternating(reach), 0.0)
    last = (row == 1) & (col == cells - 1)
    first = (row == 3) & (col == 0)
    return reach.astype(F32), geometric, jnp.where(last | first, 1.0, 0.0)


def state_matrix(parts, coefs, metric):
    reach, geometric, single = parts
    return (geometric * jnp.exp(reach * coefs[0]) + single) * metric


def border_matrix(cells, coefs, after, single):
    row = iota((cells, 128), 0)
    log_ratio, beta, edge = coefs
    reach = jnp.where(after, cells - row, row + 1)
    side = jnp.where(after, 1.0, -1.0)
    geometric = side * alternating(reach) * jnp.exp(reach.astype(F32) * log_ratio)
    beside = jnp.where(reach == 1, -side, 0.0)
    return jnp.where(single, edge * beside, beta * geometric)


def rows_left(matrix):
    high = matrix.astype(BF).astype(F32)
    return jnp.where(iota(matrix.shape, 1) < 64, high, matrix - high).astype(BF)


def pick(values, index_of_lane, alphas):
    lanes = jnp.zeros((1, 128), F32)
    for n in range(values):
        lanes = jnp.where(index_of_lane == n, alphas(n), lanes)
    return lanes


def doubled(row):
    return jnp.concatenate([row, row], axis=1)


def is_odd(axis):
    return lax.rem(lax.axis_index(axis), 2) == 1


def halo_facts(near_ref, far_ref, side, fields, lines, cells):
    x = 0 if side else lines - 1
    near = is_odd("brick") == (side == 0)
    facts = jnp.where(near, near_ref[cells : cells + 8, 0:256], far_ref[cells : cells + 8, 0:256])
    alphas = facts[0:fields, 128:256]
    alpha = jnp.sum(jnp.where(iota(alphas.shape, 1) == x, alphas, 0.0), axis=1, keepdims=True)
    return alpha, doubled(facts[0:1, 0:cells]), doubled(facts[0:1, cells : 2 * cells])


def fetch(field_in, field_scr, sem):
    fields, lines = field_scr.shape[:2]

    def copies(f):
        return [pltpu.make_async_copy(field_in.at[f, x], field_scr.at[f, x], sem.at[f, x]) for x in range(lines)]

    for f in range(AHEAD):
        for copy in copies(f):
            copy.start()

    def ready(f):
        for copy in copies(f):
            copy.wait()

        @pl.when(f + AHEAD < fields)
        def _():
            for copy in copies(f + AHEAD):
                copy.start()

    return ready


def fetch_small(pairs, sem):
    copies = [pltpu.make_async_copy(source, target, sem.at[n]) for n, (source, target) in enumerate(pairs)]
    for copy in copies:
        copy.start()
    return copies


def pack_kernel(
    alpha_in, inner_in, outer_in, field_in, near_ref, far_ref, alpha_ref, inner_ref, outer_ref, sem
):
    fields, lines = alpha_ref.shape
    cells = inner_ref.shape[1]
    odd = is_odd("brick")
    near_x = jnp.where(odd, 0, lines - 1)
    copies = fetch_small(
        [
            (alpha_in, alpha_ref),
            (inner_in, inner_ref),
            (outer_in, outer_ref),
            (field_in.at[0, near_x], near_ref.at[pl.ds(0, cells)]),
            (field_in.at[0, lines - 1 - near_x], far_ref.at[pl.ds(0, cells)]),
        ],
        sem,
    )
    for copy in copies:
        copy.wait()
    metrics = jnp.concatenate([inner_ref[...], outer_ref[...]], axis=1)
    for ref, low in ((near_ref, odd), (far_ref, jnp.logical_not(odd))):
        ref[cells:] = jnp.zeros_like(ref[cells:])
        ref[cells : cells + 1, 0 : 2 * cells] = jnp.where(low, metrics[0:1], metrics[lines - 1 :])
        ref[cells : cells + fields, 128 : 128 + lines] = alpha_ref[...]


def open_kernel(
    alpha_ref, inner_ref, outer_ref, field_in,
    part_ref, own_ref, next_ref, edge_ref, line_near_ref, line_far_ref, field_ref, first_scr, local_scr, field_sem,
):
    fields, lines, cells = field_ref.shape[:3]
    odd = is_odd("brick")
    ready = fetch(field_in, field_ref, field_sem)
    parts = local_parts(cells)
    states = state_parts(cells)

    def put(ref, f, x, rows):
        ref[f, 2 * x : 2 * x + 2] = rows[0:2]
        ref[f, 2 * (lines + x) : 2 * (lines + x) + 2] = rows[2:4]

    @pl.loop(0, fields)
    def _(f):
        coefs = coefs_of(alpha_column(alpha_ref[pl.ds(f, 1)]))
        ready(f)

        def left(x, metric):
            local = left_side(local_scr[x] * metric)
            return jnp.concatenate([local, left_side(state_matrix(states, at(coefs, x), metric))], axis=0)

        for x in range(lines):
            local_scr[x] = local_matrix(parts, at(coefs, x))
            rows = dot(left(x, doubled(inner_ref[x : x + 1])), right_side(field_ref[f, x]))
            first_scr[x] = rows[:cells]
            put(own_ref, f, x, rows[cells:])
        for x in range(lines):
            middle = (1.0 + 2.0 * SMOOTH) * first_scr[x]
            if x > 0:
                middle = middle - SMOOTH * first_scr[x - 1]
            if x < lines - 1:
                middle = middle - SMOOTH * first_scr[x + 1]
            rows = dot(left(x, doubled(outer_ref[x : x + 1])), right_side(middle))
            part_ref[f, x] = rows[:cells]
            put(next_ref, f, x, rows[cells:])
        edge_ref[f, 0] = first_scr[0]
        edge_ref[f, 1] = first_scr[lines - 1]

    for f in range(1, fields):
        low, high = field_ref[f, 0], field_ref[f, lines - 1]
        line_near_ref[f - 1] = jnp.where(odd, low, high)
        line_far_ref[f - 1] = jnp.where(odd, high, low)


def corner_kernel(
    near_x_ref, far_x_ref, outer_ref, edge_ref, own_ref, next_ref, near_ref, far_ref, ahead_ref, back_ref
):
    fields, cells, lines = edge_ref.shape[0], edge_ref.shape[2], own_ref.shape[1] // 4
    half = 2 * lines
    states = state_parts(cells)
    odd = is_odd("gz")
    for f in range(fields):
        for ref, start in ((ahead_ref, 0), (back_ref, half)):
            ref[f, 0:half] = own_ref[f, start : start + half]
            ref[f, half : 2 * half] = next_ref[f, start : start + half]
            ref[f, 2 * half + 4 :] = jnp.zeros_like(ref[f, 2 * half + 4 :])
            if 2 * f < lines:
                ref[f, 2 * half + 4 :, 0:cells] = outer_ref[2 * f : 2 * f + 2]
    for side in range(2):
        alphas, _, metric = halo_facts(near_x_ref, far_x_ref, side, fields, lines, cells)
        coefs = coefs_of(alphas)
        place = 2 * half + 2 * side
        for f in range(fields):
            matrix = state_matrix(states, at(coefs, f), -SMOOTH * metric)
            rows = dot(left_side(matrix), right_side(edge_ref[f, side]))
            ahead_ref[f, place : place + 2] = rows[0:2]
            back_ref[f, place : place + 2] = rows[2:4]
        for ref in (ahead_ref, back_ref):
            ref[fields - 1, 2 * half + 4 + side : 2 * half + 5 + side, 0:cells] = metric[:, 0:cells]
    near_ref[...] = jnp.where(odd, back_ref[...], ahead_ref[...])
    far_ref[...] = jnp.where(odd, ahead_ref[...], back_ref[...])


def border_lanes(lines, cells, alphas):
    k = iota((1, 128), 1) & 31
    line = (k & 15) >> 1
    lane_coefs = coefs_of(pick(lines, line, lambda x: alphas[x : x + 1]))
    return border_matrix(cells, lane_coefs, k >= 16, (k & 1) == 1), line, k >= 16


def spread(line, x):
    beside = (line == x - 1) | (line == x + 1)
    return jnp.where(line == x, 1.0 + 2.0 * SMOOTH, jnp.where(beside, -SMOOTH, 0.0))


def four_pieces(states):
    high, low = split(states)
    return jnp.concatenate([high, low, high, low], axis=0)


def join_kernel(
    alpha_ref, near_x_ref, far_x_ref, own_ref, near_ref, far_ref,
    first_ref, second_ref, near_out_ref, far_out_ref, behind_scr, beyond_scr,
):
    fields, lines = alpha_ref.shape
    half, cells = 2 * lines, near_x_ref.shape[0] - 8
    states = state_parts(cells)
    odd_z, odd_x = is_odd("gz"), is_odd("brick")
    behind_scr[...] = jnp.where(odd_z, near_ref[...], far_ref[...])
    beyond_scr[...] = jnp.where(odd_z, far_ref[...], near_ref[...])
    halo = [halo_facts(near_x_ref, far_x_ref, side, fields, lines, cells)[0] for side in range(2)]

    def metric_of(ref, line):
        f, row = (line // 2, line % 2) if line < lines else (fields - 1, line - lines)
        return doubled(ref[f, 2 * half + 4 + row : 2 * half + 5 + row, 0:cells])

    for f in range(fields):
        alphas = alpha_column(alpha_ref[f : f + 1])
        coefs = coefs_of(alphas)
        border, line, after = border_lanes(lines, cells, alphas)

        def caused(coef, place, weight):
            left = jnp.concatenate(
                [left_side(state_matrix(states, coef, metric_of(ref, place))) for ref in (behind_scr, beyond_scr)], axis=0
            )
            rows = dot(left, right_side(border * weight))
            return jnp.where(after, rows[0:2], 0.0), jnp.where(after, 0.0, rows[18:20])

        pairs = [caused(at(coefs, x), x, spread(line, x)) for x in range(lines)]
        for side, x in ((0, 0), (1, lines - 1)):
            coef = coefs_of(halo[side][f : f + 1])
            pairs.append(caused(coef, lines + side, jnp.where(line == x, -SMOOTH, 0.0)))
        pad = [jnp.zeros((4, 128), F32)]
        left = jnp.concatenate([p[0] for p in pairs] + pad + [p[1] for p in pairs] + pad, axis=0)
        added = dot(rows_left(left), four_pieces(own_ref[f]))
        rows = []
        for n, ref in enumerate((behind_scr, beyond_scr)):
            extra = added[24 * n : 24 * n + half + 4]
            first_ref[f, half * n : half * (n + 1)] = ref[f, 0:half]
            second_ref[f, half * n : half * (n + 1)] = ref[f, half : 2 * half] + extra[:half]
            rows.append((ref[f, 0:half], ref[f, 2 * half : 2 * half + 4] + extra[half:]))
        for part in range(2):
            sides = []
            for side, x in ((0, 0), (1, lines - 1)):
                start = 2 * x if part == 0 else 2 * side
                sides.append(jnp.concatenate([r[part][start : start + 2] for r in rows], axis=0))
            place = 4 * (fields * part + f)
            near_out_ref[place : place + 4] = jnp.where(odd_x, sides[0], sides[1])
            far_out_ref[place : place + 4] = jnp.where(odd_x, sides[1], sides[0])


def prepare_kernel(alpha_ref, outer_ref, near_x_ref, far_x_ref, cells_ref, rows_ref):
    fields, lines = alpha_ref.shape
    cells = outer_ref.shape[1]
    parts = local_parts(cells)
    k = iota((1, 128), 1) & 63
    own = k >= 4 * fields
    field = jnp.where(own, k - 4 * fields, k) >> 2

    @pl.loop(0, fields)
    def _(f):
        coefs = coefs_of(alpha_column(alpha_ref[pl.ds(f, 1)]))
        for side, x in ((0, 0), (1, lines - 1)):
            alphas, metric, _ = halo_facts(near_x_ref, far_x_ref, side, fields, lines, cells)
            own_alphas = jnp.sum(jnp.where(iota((fields, lines), 1) == x, alpha_ref[...], 0.0), axis=1, keepdims=True)
            alpha = jnp.sum(jnp.where(iota((fields, 1), 0) == f, alphas, 0.0), axis=0, keepdims=True)
            outer = left_side(local_matrix(parts, at(coefs, x)) * (-SMOOTH * doubled(outer_ref[x : x + 1])))
            inner = local_matrix(parts, coefs_of(alpha)) * metric
            cells_ref[f, side] = left_side(dot(outer, right_side(inner)))
            halo_lanes = pick(fields, field, lambda n: alphas[n : n + 1])
            own_lanes = pick(fields, field, lambda n: own_alphas[n : n + 1])
            border = border_matrix(cells, coefs_of(jnp.where(own, own_lanes, halo_lanes)), (k & 2) == 2, (k & 1) == 1)
            border = jnp.where(field == f, border, 0.0)
            passed = dot(outer, right_side(jnp.where(own, 0.0, border)))
            rows_ref[f, side] = left_side(passed + jnp.where(own, border, 0.0))


def border_kernel(alpha_ref, outer_ref, part_ref, first_ref, second_ref, out_ref, edge_ref, stage, sem):
    fields, lines, cells = part_ref.shape[:3]
    parts = local_parts(cells)

    def copies(f):
        return [pltpu.make_async_copy(stage.at[f, x], out_ref.at[f, x], sem.at[f, x]) for x in range(lines)]

    @pl.loop(0, fields)
    def _(f):
        alphas = alpha_column(alpha_ref[pl.ds(f, 1)])
        coefs = coefs_of(alphas)
        border, line, _ = border_lanes(lines, cells, alphas)
        direct = rows_left(border).astype(F32)
        left = []
        for x in range(lines):
            local = left_side(local_matrix(parts, at(coefs, x)) * doubled(outer_ref[x : x + 1]))
            passed = rows_left(dot(local, right_side(border * spread(line, x))))
            left.append(jnp.concatenate([passed, jnp.where(line == x, direct, 0.0).astype(BF)], axis=1))
        right = jnp.concatenate([four_pieces(first_ref[f]), four_pieces(second_ref[f])], axis=0)
        border = dot(jnp.concatenate(left, axis=0), right)
        for x in range(lines):
            value = part_ref[f, x] + border[cells * x : cells * (x + 1)]
            stage[f, x] = value
            if x == 0 or x == lines - 1:
                edge_ref[f, 0 if x == 0 else 1] = value
        for copy in copies(f):
            copy.start()

    @pl.loop(0, fields)
    def _(f):
        for copy in copies(f):
            copy.wait()


def by_side(near_ref, far_ref, index):
    odd = is_odd("brick")
    near, far = near_ref[index], far_ref[index]
    return jnp.where(odd, near, far), jnp.where(odd, far, near)


def late_kernel(
    cells_ref, rows_ref, edge_ref, near0_ref, far0_ref, near1_ref, far1_ref, near_rows_ref, far_rows_ref, _,
    out_ref, state_scr, term_scr, stage, sem,
):
    fields, cells, lines = edge_ref.shape[0], edge_ref.shape[2], out_ref.shape[1]
    copies = []
    for side, rows in enumerate(by_side(near_rows_ref, far_rows_ref, Ellipsis)):
        state_scr[...] = jnp.zeros_like(state_scr)
        state_scr[0 : 8 * fields] = rows
        left = jnp.concatenate([rows_ref[f, side] for f in range(fields)], axis=0)
        term_scr[side] = dot(left, right_side(state_scr[...]))
    for f in range(fields):
        if f == 0:
            pieces = by_side(near0_ref, far0_ref, slice(0, cells))
        else:
            pieces = by_side(near1_ref, far1_ref, f - 1)
        for side, halo in enumerate(pieces):
            term = edge_ref[f, side] + term_scr[side, cells * f : cells * (f + 1)]
            stage[f, side] = term + dot(cells_ref[f, side], right_side(halo))
            copies.append(pltpu.make_async_copy(stage.at[f, side], out_ref.at[f, side * (lines - 1)], sem.at[f, side]))
            copies[-1].start()
    for copy in copies:
        copy.wait()


WHOLE = pl.BlockSpec(memory_space=pltpu.VMEM)
ANY = pl.BlockSpec(memory_space=pl.ANY)
HBM = pl.BlockSpec(memory_space=pltpu.HBM)


def call(kernel, limit, ins, out_shape, outs=WHOLE, **options):
    def run(*args):
        return pl.pallas_call(
            kernel,
            in_specs=ins,
            out_specs=outs if isinstance(outs, list) else jax.tree.map(lambda _: outs, out_shape),
            out_shape=out_shape,
            compiler_params=pltpu.CompilerParams(vmem_limit_bytes=limit * 1024 * 1024),
            **options,
        )(*args)

    return run


def swap(axis, near, far):
    count = lax.axis_size(axis)
    ends = count if axis == "gz" else count - 1
    pairs = {"near": [(i, i + 1) for i in range(0, count - 1, 2)], "far": [(i, (i + 1) % count) for i in range(1, ends, 2)]}
    moved = {}
    for kind, value in (("far", far), ("near", near)):
        both = [p for a, b in pairs[kind] for p in ((a, b), (b, a))]
        moved[kind] = lax.ppermute(value, axis, both)
    return moved["near"], moved["far"]


def steps(grad_field, alpha_coef, metric_inner, metric_outer):
    fields, lines, cells, width = grad_field.shape

    def shape(*dims, kind=F32):
        return pltpu.VMEM(dims, kind)

    whole = jax.ShapeDtypeStruct(grad_field.shape, F32)

    states = shape(fields, 4 * lines, width)
    head, edge = shape(cells + 8, width), shape(fields - 1, cells, width)
    edges = shape(fields, 2, cells, width)
    whole_here = shape(*grad_field.shape)
    inputs = (alpha_coef, metric_inner, metric_outer, grad_field)
    near, far, alpha, inner, outer = call(
        pack_kernel,
        GRANT,
        [HBM] * 4,
        [head, head, *(shape(*a.shape) for a in inputs[:3])],
        scratch_shapes=[pltpu.SemaphoreType.DMA((5,))],
    )(*inputs)
    near0, far0 = swap("brick", near, far)
    part, own, following, first, line_near, line_far = call(
        open_kernel,
        GRANT,
        [WHOLE, WHOLE, WHOLE, HBM],
        [whole_here, states, states, edges, edge, edge],
        scratch_shapes=[
            pltpu.VMEM(grad_field.shape, F32),
            pltpu.VMEM((lines, cells, width), F32),
            pltpu.VMEM((lines, cells, 2 * cells), F32),
            pltpu.SemaphoreType.DMA((fields, lines)),
        ],
    )(alpha, inner, outer, grad_field)
    message = shape(fields, 4 * lines + 6, width)
    near, far = call(
        corner_kernel,
        8,
        [WHOLE] * 6,
        [message, message],
        scratch_shapes=[pltpu.VMEM((fields, 4 * lines + 6, width), F32)] * 2,
    )(near0, far0, outer, first, own, following)
    near_two, far_two = swap("gz", near, far)
    near1, far1 = swap("brick", line_near, line_far)

    matrices = shape(fields, 2, cells, 3 * cells, kind=BF)
    cell_matrix, row_matrix = call(prepare_kernel, 4, [WHOLE] * 4, [matrices, matrices])(alpha, outer, near0, far0)

    rows = shape(8 * fields, width)
    first, second, near, far = call(
        join_kernel,
        8,
        [WHOLE] * 6,
        [states, states, rows, rows],
        scratch_shapes=[pltpu.VMEM((fields, 4 * lines + 6, width), F32)] * 2,
    )(alpha, near0, far0, own, near_two, far_two)
    near3, far3 = swap("brick", near, far)

    out, edge = call(
        border_kernel,
        16,
        [WHOLE] * 5,
        [whole, edges],
        outs=[HBM, WHOLE],
        scratch_shapes=[pltpu.VMEM(grad_field.shape, F32), pltpu.SemaphoreType.DMA((fields, lines))],
    )(alpha, outer, part, first, second)

    return call(
        late_kernel,
        8,
        [WHOLE] * 9 + [HBM],
        whole,
        outs=HBM,
        input_output_aliases={9: 0},
        scratch_shapes=[
            pltpu.VMEM((cells, width), F32),
            pltpu.VMEM((2, fields * cells, width), F32),
            pltpu.VMEM((fields, 2, cells, width), F32),
            pltpu.SemaphoreType.DMA((fields, 2)),
        ],
    )(cell_matrix, row_matrix, edge, near0, far0, near1, far1, near3, far3, out)


def solution(mesh):
    placed = (P(None, "brick", "gz", None), P(None, "brick"), P("brick", "gz"), P("brick", "gz"))
    return jax.shard_map(steps, mesh=mesh, in_specs=placed, out_specs=P(None, "brick", "gz", None), check_vma=False)
```

```python
import jax
import jax.numpy as jnp
from jax import lax
from jax.experimental import pallas as pl
from jax.experimental.pallas import tpu as pltpu
from jax.sharding import PartitionSpec as P

SMOOTH = 0.2
BF = jnp.bfloat16
F32 = jnp.float32
GRANT = 54
CUT = 2
AHEAD = 3


def iota(shape, axis):
    return lax.broadcasted_iota(jnp.int32, shape, axis)


def alternating(exponent):
    return (1 - 2 * (exponent & 1)).astype(F32)


def split(values):
    high = values.astype(BF)
    low = (values - high.astype(F32)).astype(BF)
    return high, low


def right_side(values):
    high, low = split(values)
    return jnp.concatenate([high, low, high], axis=0)


def left_side(matrix):
    high, low = split(matrix)
    return jnp.concatenate([high, low[:, : matrix.shape[1] // 2]], axis=1)


def dot(left, right):
    return jnp.dot(left, right, preferred_element_type=F32)


def coefs_of(alpha):
    safe = jnp.where(alpha > 0.0, alpha, 0.25)
    ratio = 2.0 * safe / (1.0 + jnp.sqrt(1.0 - 4.0 * safe * safe))
    edge = (4.0 * safe - 1.0) / (12.0 * safe)
    beta = ((safe + 2.0) / 3.0 - edge) / safe
    return jnp.log(ratio), beta, edge


def alpha_column(row):
    n = row.shape[1]
    return jnp.sum(jnp.where(iota((n, n), 0) == iota((n, n), 1), row, 0.0), axis=1, keepdims=True)


def at(coefs, x):
    return tuple(c[x : x + 1] for c in coefs)


def local_parts(cells):
    row = iota((cells, 2 * cells), 0)
    col = iota((cells, 2 * cells), 1) & (cells - 1)
    step = col - row
    size = jnp.abs(step)
    sign = jnp.where(step > 0, 1.0, jnp.where(step < 0, -1.0, 0.0))
    return size.astype(F32), sign * alternating(size), jnp.where(size == 1, sign, 0.0)


def local_matrix(parts, coefs):
    size, sign, near = parts
    log_ratio, beta, edge = coefs
    return beta * (sign * jnp.exp(size * log_ratio)) - edge * near


def state_parts(cells):
    row = iota((16, 2 * cells), 0)
    col = iota((16, 2 * cells), 1) & (cells - 1)
    reach = jnp.where(row == 0, cells - 1 - col, col)
    geometric = jnp.where((row == 0) | (row == 2), alternating(reach), 0.0)
    last = (row == 1) & (col == cells - 1)
    first = (row == 3) & (col == 0)
    return reach.astype(F32), geometric, jnp.where(last | first, 1.0, 0.0)


def state_matrix(parts, coefs, metric):
    reach, geometric, single = parts
    return (geometric * jnp.exp(reach * coefs[0]) + single) * metric


def border_matrix(cells, coefs, after, single):
    row = iota((cells, 128), 0)
    log_ratio, beta, edge = coefs
    reach = jnp.where(after, cells - row, row + 1)
    side = jnp.where(after, 1.0, -1.0)
    geometric = side * alternating(reach) * jnp.exp(reach.astype(F32) * log_ratio)
    beside = jnp.where(reach == 1, -side, 0.0)
    return jnp.where(single, edge * beside, beta * geometric)


def rows_left(matrix):
    high = matrix.astype(BF).astype(F32)
    return jnp.where(iota(matrix.shape, 1) < 64, high, matrix - high).astype(BF)


def pick(values, index_of_lane, alphas):
    lanes = jnp.zeros((1, 128), F32)
    for n in range(values):
        lanes = jnp.where(index_of_lane == n, alphas(n), lanes)
    return lanes


def doubled(row):
    return jnp.concatenate([row, row], axis=1)


def is_odd(axis):
    return lax.rem(lax.axis_index(axis), 2) == 1


def halo_facts(near_ref, far_ref, side, fields, lines, cells):
    x = 0 if side else lines - 1
    near = is_odd("brick") == (side == 0)
    facts = jnp.where(near, near_ref[cells : cells + 8, 0:256], far_ref[cells : cells + 8, 0:256])
    alphas = facts[0:fields, 128:256]
    alpha = jnp.sum(jnp.where(iota(alphas.shape, 1) == x, alphas, 0.0), axis=1, keepdims=True)
    return alpha, doubled(facts[0:1, 0:cells]), doubled(facts[0:1, cells : 2 * cells])


def fetch(field_in, field_scr, sem):
    fields, lines = field_scr.shape[:2]

    def copies(f):
        return [pltpu.make_async_copy(field_in.at[f, x], field_scr.at[f, x], sem.at[f, x]) for x in range(lines)]

    for f in range(AHEAD):
        for copy in copies(f):
            copy.start()

    def ready(f):
        for copy in copies(f):
            copy.wait()

        @pl.when(f + AHEAD < fields)
        def _():
            for copy in copies(f + AHEAD):
                copy.start()

    return ready


def fetch_small(pairs, sem):
    copies = [pltpu.make_async_copy(source, target, sem.at[n]) for n, (source, target) in enumerate(pairs)]
    for copy in copies:
        copy.start()
    return copies


def pack_kernel(
    alpha_in, inner_in, outer_in, field_in, near_ref, far_ref, alpha_ref, inner_ref, outer_ref, sem
):
    fields, lines = alpha_ref.shape
    cells = inner_ref.shape[1]
    odd = is_odd("brick")
    near_x = jnp.where(odd, 0, lines - 1)
    copies = fetch_small(
        [
            (alpha_in, alpha_ref),
            (inner_in, inner_ref),
            (outer_in, outer_ref),
            (field_in.at[0, near_x], near_ref.at[pl.ds(0, cells)]),
            (field_in.at[0, lines - 1 - near_x], far_ref.at[pl.ds(0, cells)]),
        ],
        sem,
    )
    for copy in copies:
        copy.wait()
    metrics = jnp.concatenate([inner_ref[...], outer_ref[...]], axis=1)
    for ref, low in ((near_ref, odd), (far_ref, jnp.logical_not(odd))):
        ref[cells:] = jnp.zeros_like(ref[cells:])
        ref[cells : cells + 1, 0 : 2 * cells] = jnp.where(low, metrics[0:1], metrics[lines - 1 :])
        ref[cells : cells + fields, 128 : 128 + lines] = alpha_ref[...]


def open_kernel(
    alpha_ref, inner_ref, outer_ref, field_in,
    part_ref, own_ref, next_ref, edge_ref, line_near_ref, line_far_ref, tail_near_ref, tail_far_ref, field_ref, first_scr, local_scr, field_sem,
):
    fields, lines, cells = field_ref.shape[:3]
    odd = is_odd("brick")
    ready = fetch(field_in, field_ref, field_sem)
    parts = local_parts(cells)
    states = state_parts(cells)

    def put(ref, f, x, rows):
        ref[f, 2 * x : 2 * x + 2] = rows[0:2]
        ref[f, 2 * (lines + x) : 2 * (lines + x) + 2] = rows[2:4]

    @pl.loop(0, fields)
    def _(f):
        coefs = coefs_of(alpha_column(alpha_ref[pl.ds(f, 1)]))
        ready(f)

        def left(x, metric):
            local = left_side(local_scr[x] * metric)
            return jnp.concatenate([local, left_side(state_matrix(states, at(coefs, x), metric))], axis=0)

        for x in range(lines):
            local_scr[x] = local_matrix(parts, at(coefs, x))
            rows = dot(left(x, doubled(inner_ref[x : x + 1])), right_side(field_ref[f, x]))
            first_scr[x] = rows[:cells]
            put(own_ref, f, x, rows[cells:])
        for x in range(lines):
            middle = (1.0 + 2.0 * SMOOTH) * first_scr[x]
            if x > 0:
                middle = middle - SMOOTH * first_scr[x - 1]
            if x < lines - 1:
                middle = middle - SMOOTH * first_scr[x + 1]
            rows = dot(left(x, doubled(outer_ref[x : x + 1])), right_side(middle))
            part_ref[f, x] = rows[:cells]
            put(next_ref, f, x, rows[cells:])
        edge_ref[f, 0] = first_scr[0]
        edge_ref[f, 1] = first_scr[lines - 1]

    for f in range(1, fields):
        near, far, n = (line_near_ref, line_far_ref, f - 1) if f < CUT else (tail_near_ref, tail_far_ref, f - CUT)
        low, high = field_ref[f, 0], field_ref[f, lines - 1]
        near[n] = jnp.where(odd, low, high)
        far[n] = jnp.where(odd, high, low)


def corner_kernel(
    near_x_ref, far_x_ref, outer_ref, edge_ref, own_ref, next_ref, near_ref, far_ref, ahead_ref, back_ref
):
    fields, cells, lines = edge_ref.shape[0], edge_ref.shape[2], own_ref.shape[1] // 4
    half = 2 * lines
    states = state_parts(cells)
    odd = is_odd("gz")
    for f in range(fields):
        for ref, start in ((ahead_ref, 0), (back_ref, half)):
            ref[f, 0:half] = own_ref[f, start : start + half]
            ref[f, half : 2 * half] = next_ref[f, start : start + half]
            ref[f, 2 * half + 4 :] = jnp.zeros_like(ref[f, 2 * half + 4 :])
            if 2 * f < lines:
                ref[f, 2 * half + 4 :, 0:cells] = outer_ref[2 * f : 2 * f + 2]
    for side in range(2):
        alphas, _, metric = halo_facts(near_x_ref, far_x_ref, side, fields, lines, cells)
        coefs = coefs_of(alphas)
        place = 2 * half + 2 * side
        for f in range(fields):
            matrix = state_matrix(states, at(coefs, f), -SMOOTH * metric)
            rows = dot(left_side(matrix), right_side(edge_ref[f, side]))
            ahead_ref[f, place : place + 2] = rows[0:2]
            back_ref[f, place : place + 2] = rows[2:4]
        for ref in (ahead_ref, back_ref):
            ref[fields - 1, 2 * half + 4 + side : 2 * half + 5 + side, 0:cells] = metric[:, 0:cells]
    near_ref[...] = jnp.where(odd, back_ref[...], ahead_ref[...])
    far_ref[...] = jnp.where(odd, ahead_ref[...], back_ref[...])


def border_lanes(lines, cells, alphas):
    k = iota((1, 128), 1) & 31
    line = (k & 15) >> 1
    lane_coefs = coefs_of(pick(lines, line, lambda x: alphas[x : x + 1]))
    return border_matrix(cells, lane_coefs, k >= 16, (k & 1) == 1), line, k >= 16


def spread(line, x):
    beside = (line == x - 1) | (line == x + 1)
    return jnp.where(line == x, 1.0 + 2.0 * SMOOTH, jnp.where(beside, -SMOOTH, 0.0))


def four_pieces(states):
    high, low = split(states)
    return jnp.concatenate([high, low, high, low], axis=0)


def join_kernel(
    alpha_ref, near_x_ref, far_x_ref, own_ref, near_ref, far_ref,
    first_ref, second_ref, near_out_ref, far_out_ref, behind_scr, beyond_scr,
):
    fields, lines = alpha_ref.shape
    half, cells = 2 * lines, near_x_ref.shape[0] - 8
    states = state_parts(cells)
    odd_z, odd_x = is_odd("gz"), is_odd("brick")
    behind_scr[...] = jnp.where(odd_z, near_ref[...], far_ref[...])
    beyond_scr[...] = jnp.where(odd_z, far_ref[...], near_ref[...])
    halo = [halo_facts(near_x_ref, far_x_ref, side, fields, lines, cells)[0] for side in range(2)]

    def metric_of(ref, line):
        f, row = (line // 2, line % 2) if line < lines else (fields - 1, line - lines)
        return doubled(ref[f, 2 * half + 4 + row : 2 * half + 5 + row, 0:cells])

    for f in range(fields):
        alphas = alpha_column(alpha_ref[f : f + 1])
        coefs = coefs_of(alphas)
        border, line, after = border_lanes(lines, cells, alphas)

        def caused(coef, place, weight):
            left = jnp.concatenate(
                [left_side(state_matrix(states, coef, metric_of(ref, place))) for ref in (behind_scr, beyond_scr)], axis=0
            )
            rows = dot(left, right_side(border * weight))
            return jnp.where(after, rows[0:2], 0.0), jnp.where(after, 0.0, rows[18:20])

        pairs = [caused(at(coefs, x), x, spread(line, x)) for x in range(lines)]
        for side, x in ((0, 0), (1, lines - 1)):
            coef = coefs_of(halo[side][f : f + 1])
            pairs.append(caused(coef, lines + side, jnp.where(line == x, -SMOOTH, 0.0)))
        pad = [jnp.zeros((4, 128), F32)]
        left = jnp.concatenate([p[0] for p in pairs] + pad + [p[1] for p in pairs] + pad, axis=0)
        added = dot(rows_left(left), four_pieces(own_ref[f]))
        rows = []
        for n, ref in enumerate((behind_scr, beyond_scr)):
            extra = added[24 * n : 24 * n + half + 4]
            first_ref[f, half * n : half * (n + 1)] = ref[f, 0:half]
            second_ref[f, half * n : half * (n + 1)] = ref[f, half : 2 * half] + extra[:half]
            rows.append((ref[f, 0:half], ref[f, 2 * half : 2 * half + 4] + extra[half:]))
        for part in range(2):
            sides = []
            for side, x in ((0, 0), (1, lines - 1)):
                start = 2 * x if part == 0 else 2 * side
                sides.append(jnp.concatenate([r[part][start : start + 2] for r in rows], axis=0))
            place = 4 * (fields * part + f)
            near_out_ref[place : place + 4] = jnp.where(odd_x, sides[0], sides[1])
            far_out_ref[place : place + 4] = jnp.where(odd_x, sides[1], sides[0])


def prepare_kernel(alpha_ref, outer_ref, near_x_ref, far_x_ref, cells_ref, rows_ref):
    fields, lines = alpha_ref.shape
    cells = outer_ref.shape[1]
    parts = local_parts(cells)
    k = iota((1, 128), 1) & 63
    own = k >= 4 * fields
    field = jnp.where(own, k - 4 * fields, k) >> 2

    @pl.loop(0, fields)
    def _(f):
        coefs = coefs_of(alpha_column(alpha_ref[pl.ds(f, 1)]))
        for side, x in ((0, 0), (1, lines - 1)):
            alphas, metric, _ = halo_facts(near_x_ref, far_x_ref, side, fields, lines, cells)
            own_alphas = jnp.sum(jnp.where(iota((fields, lines), 1) == x, alpha_ref[...], 0.0), axis=1, keepdims=True)
            alpha = jnp.sum(jnp.where(iota((fields, 1), 0) == f, alphas, 0.0), axis=0, keepdims=True)
            outer = left_side(local_matrix(parts, at(coefs, x)) * (-SMOOTH * doubled(outer_ref[x : x + 1])))
            inner = local_matrix(parts, coefs_of(alpha)) * metric
            cells_ref[f, side] = left_side(dot(outer, right_side(inner)))
            halo_lanes = pick(fields, field, lambda n: alphas[n : n + 1])
            own_lanes = pick(fields, field, lambda n: own_alphas[n : n + 1])
            border = border_matrix(cells, coefs_of(jnp.where(own, own_lanes, halo_lanes)), (k & 2) == 2, (k & 1) == 1)
            border = jnp.where(field == f, border, 0.0)
            passed = dot(outer, right_side(jnp.where(own, 0.0, border)))
            rows_ref[f, side] = left_side(passed + jnp.where(own, border, 0.0))


def border_kernel(alpha_ref, outer_ref, part_ref, first_ref, second_ref, out_ref, edge_ref, stage, sem):
    fields, lines, cells = part_ref.shape[:3]
    parts = local_parts(cells)

    def copies(f):
        return [pltpu.make_async_copy(stage.at[f, x], out_ref.at[f, x], sem.at[f, x]) for x in range(lines)]

    @pl.loop(0, fields)
    def _(f):
        alphas = alpha_column(alpha_ref[pl.ds(f, 1)])
        coefs = coefs_of(alphas)
        border, line, _ = border_lanes(lines, cells, alphas)
        direct = rows_left(border).astype(F32)
        left = []
        for x in range(lines):
            local = left_side(local_matrix(parts, at(coefs, x)) * doubled(outer_ref[x : x + 1]))
            passed = rows_left(dot(local, right_side(border * spread(line, x))))
            left.append(jnp.concatenate([passed, jnp.where(line == x, direct, 0.0).astype(BF)], axis=1))
        right = jnp.concatenate([four_pieces(first_ref[f]), four_pieces(second_ref[f])], axis=0)
        border = dot(jnp.concatenate(left, axis=0), right)
        for x in range(lines):
            value = part_ref[f, x] + border[cells * x : cells * (x + 1)]
            stage[f, x] = value
            if x == 0 or x == lines - 1:
                edge_ref[f, 0 if x == 0 else 1] = value
        for copy in copies(f):
            copy.start()

    @pl.loop(0, fields)
    def _(f):
        for copy in copies(f):
            copy.wait()


def by_side(near_ref, far_ref, index):
    odd = is_odd("brick")
    near, far = near_ref[index], far_ref[index]
    return jnp.where(odd, near, far), jnp.where(odd, far, near)


def late_kernel(
    cells_ref, rows_ref, edge_ref, near0_ref, far0_ref, near1_ref, far1_ref, near2_ref, far2_ref, near_rows_ref, far_rows_ref, _,
    out_ref, state_scr, term_scr, stage, sem,
):
    fields, cells, lines = edge_ref.shape[0], edge_ref.shape[2], out_ref.shape[1]
    copies = []
    for side, rows in enumerate(by_side(near_rows_ref, far_rows_ref, Ellipsis)):
        state_scr[...] = jnp.zeros_like(state_scr)
        state_scr[0 : 8 * fields] = rows
        left = jnp.concatenate([rows_ref[f, side] for f in range(fields)], axis=0)
        term_scr[side] = dot(left, right_side(state_scr[...]))
    for f in range(fields):
        if f == 0:
            pieces = by_side(near0_ref, far0_ref, slice(0, cells))
        else:
            pieces = by_side(near1_ref, far1_ref, f - 1) if f < CUT else by_side(near2_ref, far2_ref, f - CUT)
        for side, halo in enumerate(pieces):
            term = edge_ref[f, side] + term_scr[side, cells * f : cells * (f + 1)]
            stage[f, side] = term + dot(cells_ref[f, side], right_side(halo))
            copies.append(pltpu.make_async_copy(stage.at[f, side], out_ref.at[f, side * (lines - 1)], sem.at[f, side]))
            copies[-1].start()
    for copy in copies:
        copy.wait()


WHOLE = pl.BlockSpec(memory_space=pltpu.VMEM)
ANY = pl.BlockSpec(memory_space=pl.ANY)
HBM = pl.BlockSpec(memory_space=pltpu.HBM)


def call(kernel, limit, ins, out_shape, outs=WHOLE, **options):
    def run(*args):
        return pl.pallas_call(
            kernel,
            in_specs=ins,
            out_specs=outs if isinstance(outs, list) else jax.tree.map(lambda _: outs, out_shape),
            out_shape=out_shape,
            compiler_params=pltpu.CompilerParams(vmem_limit_bytes=limit * 1024 * 1024),
            **options,
        )(*args)

    return run


def swap(axis, near, far):
    count = lax.axis_size(axis)
    ends = count if axis == "gz" else count - 1
    pairs = {"near": [(i, i + 1) for i in range(0, count - 1, 2)], "far": [(i, (i + 1) % count) for i in range(1, ends, 2)]}
    moved = {}
    for kind, value in (("far", far), ("near", near)):
        both = [p for a, b in pairs[kind] for p in ((a, b), (b, a))]
        moved[kind] = lax.ppermute(value, axis, both)
    return moved["near"], moved["far"]


def steps(grad_field, alpha_coef, metric_inner, metric_outer):
    fields, lines, cells, width = grad_field.shape

    def shape(*dims, kind=F32):
        return pltpu.VMEM(dims, kind)

    whole = jax.ShapeDtypeStruct(grad_field.shape, F32)

    states = shape(fields, 4 * lines, width)
    head, edge, tail = shape(cells + 8, width), shape(CUT - 1, cells, width), shape(fields - CUT, cells, width)
    edges = shape(fields, 2, cells, width)
    whole_here = shape(*grad_field.shape)
    inputs = (alpha_coef, metric_inner, metric_outer, grad_field)
    near, far, _, _, _ = call(
        pack_kernel,
        GRANT,
        [HBM] * 4,
        [head, head, *(shape(*a.shape) for a in inputs[:3])],
        scratch_shapes=[pltpu.SemaphoreType.DMA((5,))],
    )(*inputs)
    near0, far0 = swap("brick", near, far)
    part, own, following, first, line_near, line_far, tail_near, tail_far = call(
        open_kernel,
        GRANT - 2,
        [WHOLE, WHOLE, WHOLE, HBM],
        [whole_here, states, states, edges, edge, edge, tail, tail],
        scratch_shapes=[
            pltpu.VMEM(grad_field.shape, F32),
            pltpu.VMEM((lines, cells, width), F32),
            pltpu.VMEM((lines, cells, 2 * cells), F32),
            pltpu.SemaphoreType.DMA((fields, lines)),
        ],
    )(alpha_coef, metric_inner, metric_outer, grad_field)
    message = shape(fields, 4 * lines + 6, width)
    near, far = call(
        corner_kernel,
        8,
        [WHOLE] * 6,
        [message, message],
        scratch_shapes=[pltpu.VMEM((fields, 4 * lines + 6, width), F32)] * 2,
    )(near0, far0, metric_outer, first, own, following)
    near_two, far_two = swap("gz", near, far)
    near1, far1 = swap("brick", line_near, line_far)
    near2, far2 = swap("brick", tail_near, tail_far)

    matrices = shape(fields, 2, cells, 3 * cells, kind=BF)
    cell_matrix, row_matrix = call(prepare_kernel, 4, [WHOLE] * 4, [matrices, matrices])(alpha_coef, metric_outer, near0, far0)

    rows = shape(8 * fields, width)
    first, second, near, far = call(
        join_kernel,
        8,
        [WHOLE] * 6,
        [states, states, rows, rows],
        scratch_shapes=[pltpu.VMEM((fields, 4 * lines + 6, width), F32)] * 2,
    )(alpha_coef, near0, far0, own, near_two, far_two)
    near3, far3 = swap("brick", near, far)

    out, edge = call(
        border_kernel,
        16,
        [WHOLE] * 5,
        [whole, edges],
        outs=[HBM, WHOLE],
        scratch_shapes=[pltpu.VMEM(grad_field.shape, F32), pltpu.SemaphoreType.DMA((fields, lines))],
    )(alpha_coef, metric_outer, part, first, second)

    return call(
        late_kernel,
        8,
        [WHOLE] * 11 + [HBM],
        whole,
        outs=HBM,
        input_output_aliases={11: 0},
        scratch_shapes=[
            pltpu.VMEM((cells, width), F32),
            pltpu.VMEM((2, fields * cells, width), F32),
            pltpu.VMEM((fields, 2, cells, width), F32),
            pltpu.SemaphoreType.DMA((fields, 2)),
        ],
    )(cell_matrix, row_matrix, edge, near0, far0, near1, far1, near2, far2, near3, far3, out)


def solution(mesh):
    placed = (P(None, "brick", "gz", None), P(None, "brick"), P("brick", "gz"), P("brick", "gz"))
    return jax.shard_map(steps, mesh=mesh, in_specs=placed, out_specs=P(None, "brick", "gz", None), check_vma=False)
```
